32 devices in a mesh: lat: 4 (over x, core), lon: 8 (over z, y).
Axes of the slice: x: 2, y: 2, z: 4, core: 2. Of those that a mesh axis runs over, the one named last changes fastest.
Arguments:
- northward_volume_flux: bfloat16 [75, 1024, 1024], P(None, 'lat', 'lon'), may hold values from -6 to 6
- sheet_warmth: bfloat16 [75, 1024, 1024], P(None, 'lat', 'lon'), may hold values from -6 to 6
- ocean_region_ids: int32 [1024, 1024], P('lat', 'lon'), may hold values from 0 to 4
- ocean_grid_flags: int32 [1024, 1024], P('lat', 'lon'), may hold values 0 or 1
- thick_sheet_tally: int32 [1024, 1024], P('lat', 'lon'), may hold values from 1 to 75
Outputs:
- stream_layers: float32 [5, 75, 1024], P(None, None, 'lat')
- stream_north: float32 [5, 75, 1024], P(None, None, 'lat')
- heat_layers: float32 [5, 75, 1024], P(None, None, 'lat')
The draws below stay inside these ranges and needn't reach their ends.
All inputs are finite; a program needn't handle non-finite values. No bound on the sum of `ocean_grid_flags` on one device may be relied on, other than what follows from the above.
Results may differ from the reference program's by a relative error of at most 0.0003.
Values may be sent and summed in bfloat16 or wider, within the bound.
A program may use at most 64 MiB of HBM per device.

```python
import math
import jax
import jax.numpy as jnp
from jax import lax

ISOPYCNAL_SHEETS = 75
BASINS = 5
PARALLEL_TOTAL = 1024
MERIDIAN_TOTAL = 1024


def set_ends(result, rng, least, high):
    place = [jax.random.randint(jax.random.fold_in(rng, axis), (), 0, length) for axis, length in enumerate(result.shape)]
    longest = result.shape.index(max(result.shape))
    next_to = place[:longest] + [(place[longest] + 1) % result.shape[longest]] + place[longest + 1:]
    return result.at[tuple(place)].set(least).at[tuple(next_to)].set(high)


def levels(key, extent, cuts, least, largest):
    level = 1.0
    for axis_at, parts in cuts:
        heights = jax.random.uniform(jax.random.fold_in(jax.random.fold_in(key, 6), axis_at), (parts,), jnp.float32, least / len(cuts), largest / len(cuts))
        level = level * jnp.repeat(jnp.exp(heights), extent[axis_at] // parts).reshape((-1,) + (1,) * (len(extent) - 1 - axis_at))
    return level


def bell_draw(stream_key, dims, scale, most, shards=(), held_as=jnp.bfloat16):
    level = levels(stream_key, dims, shards, -0.22, 0.18) if shards else 1.0
    drawn = jax.random.normal(stream_key, dims, jnp.float32) * scale * level
    return jnp.minimum(jnp.maximum(drawn, -most), most).astype(held_as)


def setup_inputs(seed: int = 0) -> dict:
    keys = jax.random.split(jax.random.key(seed), 6)
    northward_volume_flux = bell_draw(keys[0], (ISOPYCNAL_SHEETS, PARALLEL_TOTAL, MERIDIAN_TOTAL), 1.0, 6.0, ((1, 4), (2, 8)))
    sheet_warmth = bell_draw(keys[1], (ISOPYCNAL_SHEETS, PARALLEL_TOTAL, MERIDIAN_TOTAL), 1.0, 6.0, ((1, 4), (2, 8)))
    ocean_region_ids = set_ends(jax.random.randint(keys[2], (PARALLEL_TOTAL, MERIDIAN_TOTAL), 0, BASINS), jax.random.fold_in(keys[2], 1), 0, BASINS - 1).astype(jnp.int32)
    ocean_grid_flags = set_ends((jax.random.randint(keys[3], (PARALLEL_TOTAL, MERIDIAN_TOTAL), 0, 4) < 3).astype(jnp.int32), jax.random.fold_in(keys[3], 1), 0, 1)
    thick_sheet_tally = set_ends(jax.random.randint(keys[4], (PARALLEL_TOTAL, MERIDIAN_TOTAL), 1, ISOPYCNAL_SHEETS + 1), jax.random.fold_in(keys[4], 1), 1, ISOPYCNAL_SHEETS).astype(jnp.int32)
    return {"northward_volume_flux": northward_volume_flux, "sheet_warmth": sheet_warmth, "ocean_region_ids": ocean_region_ids, "ocean_grid_flags": ocean_grid_flags, "thick_sheet_tally": thick_sheet_tally}


def reference(northward_volume_flux, sheet_warmth, ocean_region_ids, ocean_grid_flags, thick_sheet_tally):
    level = jnp.arange(ISOPYCNAL_SHEETS, dtype=jnp.int32)[:, None, None]
    live_cells = ocean_grid_flags[None].astype(jnp.float32) * (level < thick_sheet_tally[None]).astype(jnp.float32)
    flow = northward_volume_flux.astype(jnp.float32) * live_cells
    centre_warmth = sheet_warmth.astype(jnp.float32)
    upper_neighbour = jnp.concatenate([centre_warmth[:, 1:, :], jnp.zeros((ISOPYCNAL_SHEETS, 1, MERIDIAN_TOTAL), jnp.float32)], axis=1)
    interface_warmth = 0.5 * (centre_warmth + upper_neighbour)
    basin_table = (ocean_region_ids[:, :, None] == jnp.arange(BASINS, dtype=jnp.int32)[None, None, :]).astype(jnp.float32)
    scale_x = 1.0 / math.sqrt(MERIDIAN_TOTAL)
    zonal_flow = jnp.einsum('kyx,yxb->bky', flow, basin_table, precision=lax.Precision.HIGHEST) * scale_x
    heat_layers = jnp.einsum('kyx,yxb->bky', flow * interface_warmth, basin_table, precision=lax.Precision.HIGHEST) * scale_x
    stream_layers = jnp.cumsum(zonal_flow, axis=1) * (1.0 / math.sqrt(ISOPYCNAL_SHEETS))
    stream_north = jnp.cumsum(stream_layers, axis=2) * (1.0 / math.sqrt(PARALLEL_TOTAL))
    return (stream_layers, stream_north, heat_layers)
```

```python
import functools
import math

import jax
import jax.numpy as jnp
from jax import lax
from jax.experimental import pallas as pl
from jax.experimental.pallas import tpu as pltpu
from jax.sharding import PartitionSpec as P

BASINS = 5
GROUP = 8
F32, BF16 = jnp.float32, jnp.bfloat16


def nt_dot(a, b):
    return lax.dot_general(a, b, (((1,), (1,)), ((), ())), preferred_element_type=F32)


def split(x):
    high = x.astype(BF16)
    return high, (x - high.astype(F32)).astype(BF16)


def kernel(
    n_lat, n_lon, layers, scales,
    flux_hbm, warm_hbm, ids_ref, flags_ref, tally_ref,
    stream_out, north_out, heat_out,
    flux, warm, masks, live_tally, acc, landed, reduced, strip, zonal, totals, every,
    in_sem, rs_send, rs_recv, ag_send, ag_recv, strip_send, strip_recv, tot_send, tot_recv,
):
    scale_x, scale_layers, scale_y = scales
    rows, columns = ids_ref.shape
    groups = flux.shape[0] // GROUP
    planes = 2 * BASINS
    depth = landed.shape[1]
    me_lat = lax.axis_index("lat")
    me = lax.axis_index("lon")

    loads = []
    for g in range(groups):
        size = min(GROUP, layers - g * GROUP)
        part = pl.ds(g * GROUP, size)
        pair = (
            pltpu.make_async_copy(flux_hbm.at[part], flux.at[part], in_sem.at[0, g]),
            pltpu.make_async_copy(warm_hbm.at[part], warm.at[part], in_sem.at[1, g]),
        )
        for copy in pair:
            copy.start()
        loads.append(pair)

    barrier = pltpu.get_barrier_semaphore()
    for j in range(1, n_lon):
        pl.semaphore_signal(
            barrier, inc=1, device_id={"lon": lax.rem(me + j, n_lon)},
            device_id_type=pl.DeviceIdType.MESH,
        )
    for j in range(1, n_lat):
        pl.semaphore_signal(
            barrier, inc=1, device_id={"lat": lax.rem(me_lat + j, n_lat)},
            device_id_type=pl.DeviceIdType.MESH,
        )

    spare = groups * GROUP - layers
    if spare:
        flux[pl.ds(layers, spare)] = jnp.zeros((spare, rows, columns), BF16)
        warm[pl.ds(layers, spare)] = jnp.zeros((spare, rows, columns), BF16)
    left = acc.shape[0] - groups * planes
    if left:
        acc[pl.ds(groups * planes, left)] = jnp.zeros((left, GROUP, rows), F32)
    ids = ids_ref[...]
    for b in range(BASINS):
        masks[b] = (ids == b).astype(F32).astype(BF16)
    live_tally[...] = flags_ref[...] * tally_ref[...]

    pl.semaphore_wait(barrier, n_lon - 1 + n_lat - 1)
    strip_copy = pltpu.make_async_remote_copy(
        src_ref=warm_hbm.at[:, pl.ds(0, 8), :], dst_ref=strip,
        send_sem=strip_send, recv_sem=strip_recv,
        device_id={"lat": lax.rem(me_lat + n_lat - 1, n_lat)},
        device_id_type=pl.DeviceIdType.MESH,
    )
    pl.when(me_lat > 0)(strip_copy.start)

    last_row = lax.broadcasted_iota(jnp.int32, (rows, columns), 0) == rows - 1
    lane_half = lax.broadcasted_iota(jnp.int32, (GROUP, 2 * columns), 1) // columns
    slot = lax.broadcasted_iota(jnp.int32, (GROUP, 2 * columns), 0)

    def one_group(g, carry):
        zsum = [jnp.zeros((GROUP, rows), F32) for _ in range(BASINS)]
        hsum = [jnp.zeros((GROUP, rows), F32) for _ in range(BASINS)]
        for pair in range(GROUP // 2):
            held = []
            for half in range(2):
                i = 2 * pair + half
                k = g * GROUP + i
                live = k < live_tally[...]
                f = jnp.where(live, flux[k].astype(F32), 0.0)
                t = warm[k].astype(F32)
                up = jnp.where(last_row, 0.0, pltpu.roll(t, rows - 1, 0))
                high, low = split(f * (t + up))
                fb = f.astype(BF16)
                held.append(fb)
                pick = (slot == i).astype(F32).astype(BF16)
                for b in range(BASINS):
                    m = masks[b]
                    hsum[b] += nt_dot(pick, jnp.concatenate([high * m, low * m], axis=1))
            pick = (slot == 2 * pair + lane_half).astype(F32).astype(BF16)
            for b in range(BASINS):
                m = masks[b]
                zsum[b] += nt_dot(pick, jnp.concatenate([held[0] * m, held[1] * m], axis=1))
        for b in range(BASINS):
            acc[g * planes + b] = zsum[b] * scale_x
            acc[g * planes + BASINS + b] = hsum[b] * (0.5 * scale_x)
        return carry

    for pair in loads:
        for copy in pair:
            copy.wait()
    lax.fori_loop(0, groups, one_group, 0)

    @pl.when(me_lat < n_lat - 1)
    def _():
        strip_copy.wait_recv()
        near = strip[...].astype(F32)[:, 0, :]
        mine = flux[pl.ds(0, layers), pl.ds(rows - 16, 16), :].astype(F32)[:, 15, :]
        level = lax.broadcasted_iota(jnp.int32, (layers, columns), 0)
        tall = live_tally[pl.ds(rows - 1, 1), :]
        extra = jnp.where(level < tall, near * mine, 0.0) * (0.5 * scale_x)
        last = ids_ref[pl.ds(rows - 1, 1), :]
        end = lax.broadcasted_iota(jnp.int32, (GROUP, rows), 1) == rows - 1
        for b in range(BASINS):
            column = jnp.sum(jnp.where(last == b, extra, 0.0), axis=1, keepdims=True)
            if spare:
                column = jnp.concatenate([column, jnp.zeros((spare, 1), F32)], axis=0)
            for g in range(groups):
                at = g * planes + BASINS + b
                piece = column[g * GROUP:(g + 1) * GROUP]
                acc[at] = acc[at] + jnp.where(end, piece, 0.0)

    def to_lon(peer, src, dst, send, recv):
        return pltpu.make_async_remote_copy(
            src_ref=src, dst_ref=dst, send_sem=send, recv_sem=recv,
            device_id={"lon": peer}, device_id_type=pl.DeviceIdType.MESH,
        )

    scatter = []
    for j in range(1, n_lon):
        peer = lax.rem(me + j, n_lon)
        copy = to_lon(
            peer, acc.at[pl.ds(peer * depth, depth)], landed.at[j], rs_send.at[j], rs_recv.at[j]
        )
        copy.start()
        scatter.append(copy)
    total = acc[pl.ds(me * depth, depth)]
    for j in range(1, n_lon):
        scatter[j - 1].wait_recv()
        total = total + landed[j]
    mine_out = reduced.at[pl.ds(me * depth, depth)]
    mine_out[...] = total
    gather = []
    for j in range(1, n_lon):
        peer = lax.rem(me + j, n_lon)
        copy = to_lon(peer, mine_out, mine_out, ag_send.at[j], ag_recv.at[j])
        copy.start()
        gather.append(copy)
    for j in range(1, n_lon):
        gather[j - 1].wait_recv()

    sub = lax.broadcasted_iota(jnp.int32, (GROUP, rows), 0)
    for b in range(BASINS):
        above = jnp.zeros((1, rows), F32)
        for g in range(groups):
            x = reduced[g * planes + b]
            for by in (1, 2, 4):
                x = x + jnp.where(sub >= by, pltpu.roll(x, by, 0), 0.0)
            x = x + above
            above = x[GROUP - 1:GROUP]
            zonal[pl.ds((b * groups + g) * GROUP, GROUP), :] = x * scale_layers
    used = BASINS * groups * GROUP
    padded = zonal.shape[0]
    if padded > used:
        zonal[pl.ds(used, padded - used), :] = jnp.zeros((padded - used, rows), F32)
    high, low = split(zonal[...])
    ones = jnp.ones((GROUP, rows), BF16)
    totals[...] = nt_dot(ones, high) + nt_dot(ones, low)
    sends = []
    for j in range(1, n_lat):
        copy = pltpu.make_async_remote_copy(
            src_ref=totals, dst_ref=every.at[j], send_sem=tot_send.at[j], recv_sem=tot_recv.at[j],
            device_id={"lat": lax.rem(me_lat + j, n_lat)}, device_id_type=pl.DeviceIdType.MESH,
        )
        copy.start()
        sends.append(copy)
    upper = (
        lax.broadcasted_iota(jnp.int32, (rows, rows), 0)
        <= lax.broadcasted_iota(jnp.int32, (rows, rows), 1)
    ).astype(F32).astype(BF16)
    running = jnp.dot(high, upper, preferred_element_type=F32) + jnp.dot(
        low, upper, preferred_element_type=F32
    )
    height = groups * GROUP
    for b in range(BASINS):
        stream_out[b] = zonal[pl.ds(b * height, layers), :]
        for g in range(groups):
            size = min(GROUP, layers - g * GROUP)
            heat_out[b, pl.ds(g * GROUP, size), :] = reduced[g * planes + BASINS + b][:size]
    carried = jnp.zeros((GROUP, padded), F32)
    for j in range(1, n_lat):
        sends[j - 1].wait_recv()
        carried = carried + jnp.where(me_lat >= j, every[j], 0.0)
    blocks = []
    for i in range(padded // 128):
        line = carried[0:1, i * 128:(i + 1) * 128]
        blocks.append(jnp.broadcast_to(line, (128, 128)).T)
    spread = jnp.concatenate(blocks, axis=0)
    spread = jnp.concatenate([spread] * (rows // 128), axis=1)
    zonal[...] = (running + spread) * scale_y
    for b in range(BASINS):
        north_out[b] = zonal[pl.ds(b * height, layers), :]

    pl.when(me_lat > 0)(strip_copy.wait_send)
    for copy in scatter + gather + sends:
        copy.wait_send()


def on_device(
    northward_volume_flux, sheet_warmth, ocean_region_ids, ocean_grid_flags, thick_sheet_tally
):
    layers, rows, columns = northward_volume_flux.shape
    n_lat, n_lon = lax.axis_size("lat"), lax.axis_size("lon")
    scales = (
        1.0 / math.sqrt(columns * n_lon), 1.0 / math.sqrt(layers), 1.0 / math.sqrt(rows * n_lat)
    )
    groups = -(-layers // GROUP)
    tiles = groups * 2 * BASINS
    depth = -(-tiles // n_lon)
    padded = -(-BASINS * groups * GROUP // 128) * 128
    out = jax.ShapeDtypeStruct((BASINS, layers, rows), F32)
    anywhere = pl.BlockSpec(memory_space=pl.ANY)
    inside = pl.BlockSpec(memory_space=pltpu.VMEM)
    dma = pltpu.SemaphoreType.DMA
    return pl.pallas_call(
        functools.partial(kernel, n_lat, n_lon, layers, scales),
        out_shape=(out, out, out),
        in_specs=[anywhere, anywhere, inside, inside, inside],
        out_specs=(inside, inside, inside),
        scratch_shapes=[
            pltpu.VMEM((groups * GROUP, rows, columns), BF16),
            pltpu.VMEM((groups * GROUP, rows, columns), BF16),
            pltpu.VMEM((BASINS, rows, columns), BF16),
            pltpu.VMEM((rows, columns), jnp.int32),
            pltpu.VMEM((n_lon * depth, GROUP, rows), F32),
            pltpu.VMEM((n_lon, depth, GROUP, rows), F32),
            pltpu.VMEM((n_lon * depth, GROUP, rows), F32),
            pltpu.VMEM((layers, 8, columns), BF16),
            pltpu.VMEM((padded, rows), F32),
            pltpu.VMEM((GROUP, padded), F32),
            pltpu.VMEM((n_lat, GROUP, padded), F32),
            dma((2, groups)),
            dma((n_lon,)), dma((n_lon,)), dma((n_lon,)), dma((n_lon,)),
            dma, dma,
            dma((n_lat,)), dma((n_lat,)),
        ],
        compiler_params=pltpu.CompilerParams(
            collective_id=0, has_side_effects=True, vmem_limit_bytes=60 * 1024 * 1024
        ),
        name="overturning",
    )(northward_volume_flux, sheet_warmth, ocean_region_ids, ocean_grid_flags, thick_sheet_tally)


def solution(mesh):
    placed = (
        P(None, "lat", "lon"),
        P(None, "lat", "lon"),
        P("lat", "lon"),
        P("lat", "lon"),
        P("lat", "lon"),
    )
    return jax.shard_map(
        on_device,
        mesh=mesh,
        in_specs=placed,
        out_specs=(P(None, None, "lat"), P(None, None, "lat"), P(None, None, "lat")),
        check_vma=False,
    )
```

```python
import functools
import math

import jax
import jax.numpy as jnp
from jax import lax
from jax.experimental import pallas as pl
from jax.experimental.pallas import tpu as pltpu
from jax.sharding import PartitionSpec as P

BASINS = 5
GROUP = 8
F32, BF16 = jnp.float32, jnp.bfloat16


def nt_dot(a, b):
    return lax.dot_general(a, b, (((1,), (1,)), ((), ())), preferred_element_type=F32)


def split(x):
    high = x.astype(BF16)
    return high, (x - high.astype(F32)).astype(BF16)


def kernel(
    n_lat, n_lon, layers, scales,
    flux_hbm, warm_hbm, ids_ref, flags_ref, tally_ref,
    stream_out, north_out, heat_out,
    flux, warm, masks, live_tally, acc, landed, reduced, strip, zonal, totals, every,
    in_sem, rs_send, rs_recv, ag_send, ag_recv, strip_send, strip_recv, tot_send, tot_recv,
):
    scale_x, scale_layers, scale_y = scales
    rows, columns = ids_ref.shape
    groups = flux.shape[0] // GROUP
    planes = 2 * BASINS
    depth = landed.shape[1]
    me_lat = lax.axis_index("lat")
    me = lax.axis_index("lon")

    loads = []
    for g in range(groups):
        size = min(GROUP, layers - g * GROUP)
        part = pl.ds(g * GROUP, size)
        pair = (
            pltpu.make_async_copy(flux_hbm.at[part], flux.at[part], in_sem.at[0, g]),
            pltpu.make_async_copy(warm_hbm.at[part], warm.at[part], in_sem.at[1, g]),
        )
        for copy in pair:
            copy.start()
        loads.append(pair)

    barrier = pltpu.get_barrier_semaphore()
    for j in range(1, n_lon):
        pl.semaphore_signal(
            barrier, inc=1, device_id={"lon": lax.rem(me + j, n_lon)},
            device_id_type=pl.DeviceIdType.MESH,
        )
    for j in range(1, n_lat):
        pl.semaphore_signal(
            barrier, inc=1, device_id={"lat": lax.rem(me_lat + j, n_lat)},
            device_id_type=pl.DeviceIdType.MESH,
        )

    spare = groups * GROUP - layers
    if spare:
        flux[pl.ds(layers, spare)] = jnp.zeros((spare, rows, columns), BF16)
        warm[pl.ds(layers, spare)] = jnp.zeros((spare, rows, columns), BF16)
        strip[pl.ds(layers, spare)] = jnp.zeros((spare, 8, columns), BF16)
    left = acc.shape[0] - groups * planes
    if left:
        acc[pl.ds(groups * planes, left)] = jnp.zeros((left, GROUP, rows), F32)
    ids = ids_ref[...]
    for b in range(BASINS):
        masks[b] = (ids == b).astype(F32).astype(BF16)
    live_tally[...] = flags_ref[...] * tally_ref[...]

    @pl.when(me_lat == n_lat - 1)
    def _():
        strip[pl.ds(0, layers)] = jnp.zeros((layers, 8, columns), BF16)

    pl.semaphore_wait(barrier, n_lon - 1 + n_lat - 1)
    strip_copy = pltpu.make_async_remote_copy(
        src_ref=warm_hbm.at[:, pl.ds(0, 8), :], dst_ref=strip.at[pl.ds(0, layers)],
        send_sem=strip_send, recv_sem=strip_recv,
        device_id={"lat": lax.rem(me_lat + n_lat - 1, n_lat)},
        device_id_type=pl.DeviceIdType.MESH,
    )
    pl.when(me_lat > 0)(strip_copy.start)

    last_row = lax.broadcasted_iota(jnp.int32, (rows, columns), 0) == rows - 1
    lane_half = lax.broadcasted_iota(jnp.int32, (GROUP, 2 * columns), 1) // columns
    slot = lax.broadcasted_iota(jnp.int32, (GROUP, 2 * columns), 0)

    def to_lon(peer, src, dst, send, recv):
        return pltpu.make_async_remote_copy(
            src_ref=src, dst_ref=dst, send_sem=send, recv_sem=recv,
            device_id={"lon": peer}, device_id_type=pl.DeviceIdType.MESH,
        )

    scatter = []
    for j in range(1, n_lon):
        peer = lax.rem(me + j, n_lon)
        copy = to_lon(
            peer, acc.at[pl.ds(peer * depth, depth)], landed.at[j], rs_send.at[j], rs_recv.at[j]
        )
        scatter.append(copy)
    tiles = groups * planes
    first = lax.rem(me + 1, n_lon) * depth
    start = jnp.minimum(first, tiles - 1) // planes

    def ready(peer):
        a = jnp.minimum(peer * depth, tiles - 1) // planes
        c = jnp.minimum(peer * depth + depth - 1, tiles - 1) // planes
        cut = jnp.logical_and(a < start, start <= c)
        return jnp.where(cut, groups - 1, lax.rem(c - start + groups, groups))

    def one_group(step, carry):
        g = lax.rem(start + step, groups)
        zsum = [jnp.zeros((GROUP, rows), F32) for _ in range(BASINS)]
        hsum = [jnp.zeros((GROUP, rows), F32) for _ in range(BASINS)]
        for pair in range(GROUP // 2):
            held = []
            for half in range(2):
                i = 2 * pair + half
                k = g * GROUP + i
                live = k < live_tally[...]
                f = jnp.where(live, flux[k].astype(F32), 0.0)
                t = warm[k].astype(F32)
                up = jnp.where(last_row, strip[k].astype(F32)[0:1], pltpu.roll(t, rows - 1, 0))
                high, low = split(f * (t + up))
                fb = f.astype(BF16)
                held.append(fb)
                pick = (slot == i).astype(F32).astype(BF16)
                for b in range(BASINS):
                    m = masks[b]
                    hsum[b] += nt_dot(pick, jnp.concatenate([high * m, low * m], axis=1))
            pick = (slot == 2 * pair + lane_half).astype(F32).astype(BF16)
            for b in range(BASINS):
                m = masks[b]
                zsum[b] += nt_dot(pick, jnp.concatenate([held[0] * m, held[1] * m], axis=1))
        for b in range(BASINS):
            acc[g * planes + b] = zsum[b] * scale_x
            acc[g * planes + BASINS + b] = hsum[b] * (0.5 * scale_x)
        for j in range(1, n_lon):
            pl.when(step == ready(lax.rem(me + j, n_lon)))(scatter[j - 1].start)
        return carry

    pl.when(me_lat < n_lat - 1)(strip_copy.wait_recv)
    for pair in loads:
        for copy in pair:
            copy.wait()
    lax.fori_loop(0, groups, one_group, 0)

    total = acc[pl.ds(me * depth, depth)]
    for j in range(1, n_lon):
        scatter[j - 1].wait_recv()
        total = total + landed[j]
    mine_out = reduced.at[pl.ds(me * depth, depth)]
    mine_out[...] = total
    gather = []
    for j in range(1, n_lon):
        peer = lax.rem(me + j, n_lon)
        copy = to_lon(peer, mine_out, mine_out, ag_send.at[j], ag_recv.at[j])
        copy.start()
        gather.append(copy)
    for j in range(1, n_lon):
        gather[j - 1].wait_recv()

    sub = lax.broadcasted_iota(jnp.int32, (GROUP, rows), 0)
    for b in range(BASINS):
        above = jnp.zeros((1, rows), F32)
        for g in range(groups):
            x = reduced[g * planes + b]
            for by in (1, 2, 4):
                x = x + jnp.where(sub >= by, pltpu.roll(x, by, 0), 0.0)
            x = x + above
            above = x[GROUP - 1:GROUP]
            zonal[pl.ds((b * groups + g) * GROUP, GROUP), :] = x * scale_layers
    used = BASINS * groups * GROUP
    padded = zonal.shape[0]
    if padded > used:
        zonal[pl.ds(used, padded - used), :] = jnp.zeros((padded - used, rows), F32)
    high, low = split(zonal[...])
    ones = jnp.ones((GROUP, rows), BF16)
    totals[...] = nt_dot(ones, high) + nt_dot(ones, low)
    sends = []
    for j in range(1, n_lat):
        copy = pltpu.make_async_remote_copy(
            src_ref=totals, dst_ref=every.at[j], send_sem=tot_send.at[j], recv_sem=tot_recv.at[j],
            device_id={"lat": lax.rem(me_lat + j, n_lat)}, device_id_type=pl.DeviceIdType.MESH,
        )
        copy.start()
        sends.append(copy)
    upper = (
        lax.broadcasted_iota(jnp.int32, (rows, rows), 0)
        <= lax.broadcasted_iota(jnp.int32, (rows, rows), 1)
    ).astype(F32).astype(BF16)
    running = jnp.dot(high, upper, preferred_element_type=F32) + jnp.dot(
        low, upper, preferred_element_type=F32
    )
    height = groups * GROUP
    for b in range(BASINS):
        stream_out[b] = zonal[pl.ds(b * height, layers), :]
        for g in range(groups):
            size = min(GROUP, layers - g * GROUP)
            heat_out[b, pl.ds(g * GROUP, size), :] = reduced[g * planes + BASINS + b][:size]
    carried = jnp.zeros((GROUP, padded), F32)
    for j in range(1, n_lat):
        sends[j - 1].wait_recv()
        carried = carried + jnp.where(me_lat >= j, every[j], 0.0)
    blocks = []
    for i in range(padded // 128):
        line = carried[0:1, i * 128:(i + 1) * 128]
        blocks.append(jnp.broadcast_to(line, (128, 128)).T)
    spread = jnp.concatenate(blocks, axis=0)
    spread = jnp.concatenate([spread] * (rows // 128), axis=1)
    zonal[...] = (running + spread) * scale_y
    for b in range(BASINS):
        north_out[b] = zonal[pl.ds(b * height, layers), :]

    pl.when(me_lat > 0)(strip_copy.wait_send)
    for copy in scatter + gather + sends:
        copy.wait_send()


def on_device(
    northward_volume_flux, sheet_warmth, ocean_region_ids, ocean_grid_flags, thick_sheet_tally
):
    layers, rows, columns = northward_volume_flux.shape
    n_lat, n_lon = lax.axis_size("lat"), lax.axis_size("lon")
    scales = (
        1.0 / math.sqrt(columns * n_lon), 1.0 / math.sqrt(layers), 1.0 / math.sqrt(rows * n_lat)
    )
    groups = -(-layers // GROUP)
    tiles = groups * 2 * BASINS
    depth = -(-tiles // n_lon)
    padded = -(-BASINS * groups * GROUP // 128) * 128
    out = jax.ShapeDtypeStruct((BASINS, layers, rows), F32)
    anywhere = pl.BlockSpec(memory_space=pl.ANY)
    inside = pl.BlockSpec(memory_space=pltpu.VMEM)
    dma = pltpu.SemaphoreType.DMA
    return pl.pallas_call(
        functools.partial(kernel, n_lat, n_lon, layers, scales),
        out_shape=(out, out, out),
        in_specs=[anywhere, anywhere, inside, inside, inside],
        out_specs=(inside, inside, inside),
        scratch_shapes=[
            pltpu.VMEM((groups * GROUP, rows, columns), BF16),
            pltpu.VMEM((groups * GROUP, rows, columns), BF16),
            pltpu.VMEM((BASINS, rows, columns), BF16),
            pltpu.VMEM((rows, columns), jnp.int32),
            pltpu.VMEM((n_lon * depth, GROUP, rows), F32),
            pltpu.VMEM((n_lon, depth, GROUP, rows), F32),
            pltpu.VMEM((n_lon * depth, GROUP, rows), F32),
            pltpu.VMEM((groups * GROUP, 8, columns), BF16),
            pltpu.VMEM((padded, rows), F32),
            pltpu.VMEM((GROUP, padded), F32),
            pltpu.VMEM((n_lat, GROUP, padded), F32),
            dma((2, groups)),
            dma((n_lon,)), dma((n_lon,)), dma((n_lon,)), dma((n_lon,)),
            dma, dma,
            dma((n_lat,)), dma((n_lat,)),
        ],
        compiler_params=pltpu.CompilerParams(
            collective_id=0, has_side_effects=True, vmem_limit_bytes=60 * 1024 * 1024
        ),
        name="overturning",
    )(northward_volume_flux, sheet_warmth, ocean_region_ids, ocean_grid_flags, thick_sheet_tally)


def solution(mesh):
    placed = (
        P(None, "lat", "lon"),
        P(None, "lat", "lon"),
        P("lat", "lon"),
        P("lat", "lon"),
        P("lat", "lon"),
    )
    return jax.shard_map(
        on_device,
        mesh=mesh,
        in_specs=placed,
        out_specs=(P(None, None, "lat"), P(None, None, "lat"), P(None, None, "lat")),
        check_vma=False,
    )
```

```python
import functools
import math

import jax
import jax.numpy as jnp
from jax import lax
from jax.experimental import pallas as pl
from jax.experimental.pallas import tpu as pltpu
from jax.sharding import PartitionSpec as P

BASINS = 5
GROUP = 8
F32, BF16 = jnp.float32, jnp.bfloat16


def nt_dot(a, b):
    return lax.dot_general(a, b, (((1,), (1,)), ((), ())), preferred_element_type=F32)


def split(x):
    high = x.astype(BF16)
    return high, (x - high.astype(F32)).astype(BF16)


def kernel(
    n_lat, n_lon, layers, scales,
    flux_hbm, warm_hbm, ids_ref, flags_ref, tally_ref,
    stream_out, north_out, heat_out,
    flux, warm, masks, live_tally, acc, landed, reduced, strip, zonal, totals, every,
    in_sem, rs_send, rs_recv, ag_send, ag_recv, strip_send, strip_recv, tot_send, tot_recv,
):
    scale_x, scale_layers, scale_y = scales
    rows, columns = ids_ref.shape
    groups = flux.shape[0] // GROUP
    planes = 2 * BASINS
    depth = landed.shape[1]
    me_lat = lax.axis_index("lat")
    me = lax.axis_index("lon")

    loads = []
    for g in range(groups):
        size = min(GROUP, layers - g * GROUP)
        part = pl.ds(g * GROUP, size)
        pair = (
            pltpu.make_async_copy(flux_hbm.at[part], flux.at[part], in_sem.at[0, g]),
            pltpu.make_async_copy(warm_hbm.at[part], warm.at[part], in_sem.at[1, g]),
        )
        for copy in pair:
            copy.start()
        loads.append(pair)

    barrier = pltpu.get_barrier_semaphore()
    for j in range(1, n_lon):
        pl.semaphore_signal(
            barrier, inc=1, device_id={"lon": lax.rem(me + j, n_lon)},
            device_id_type=pl.DeviceIdType.MESH,
        )
    for j in range(1, n_lat):
        pl.semaphore_signal(
            barrier, inc=1, device_id={"lat": lax.rem(me_lat + j, n_lat)},
            device_id_type=pl.DeviceIdType.MESH,
        )

    spare = groups * GROUP - layers
    if spare:
        flux[pl.ds(layers, spare)] = jnp.zeros((spare, rows, columns), BF16)
        warm[pl.ds(layers, spare)] = jnp.zeros((spare, rows, columns), BF16)
        strip[pl.ds(layers, spare)] = jnp.zeros((spare, 8, columns), BF16)
    left = acc.shape[0] - groups * planes
    if left:
        acc[pl.ds(groups * planes, left)] = jnp.zeros((left, GROUP, rows), F32)
    ids = ids_ref[...]
    for b in range(BASINS):
        masks[b] = (ids == b).astype(F32).astype(BF16)
    live_tally[...] = flags_ref[...] * tally_ref[...]

    @pl.when(me_lat == n_lat - 1)
    def _():
        strip[pl.ds(0, layers)] = jnp.zeros((layers, 8, columns), BF16)

    pl.semaphore_wait(barrier, n_lon - 1 + n_lat - 1)
    strip_copy = pltpu.make_async_remote_copy(
        src_ref=warm_hbm.at[:, pl.ds(0, 8), :], dst_ref=strip.at[pl.ds(0, layers)],
        send_sem=strip_send, recv_sem=strip_recv,
        device_id={"lat": lax.rem(me_lat + n_lat - 1, n_lat)},
        device_id_type=pl.DeviceIdType.MESH,
    )
    pl.when(me_lat > 0)(strip_copy.start)

    last_row = lax.broadcasted_iota(jnp.int32, (rows, columns), 0) == rows - 1
    lane_half = lax.broadcasted_iota(jnp.int32, (GROUP, 2 * columns), 1) // columns
    slot = lax.broadcasted_iota(jnp.int32, (GROUP, 2 * columns), 0)

    def to_lon(peer, src, dst, send, recv):
        return pltpu.make_async_remote_copy(
            src_ref=src, dst_ref=dst, send_sem=send, recv_sem=recv,
            device_id={"lon": peer}, device_id_type=pl.DeviceIdType.MESH,
        )

    scatter = []
    for j in range(1, n_lon):
        peer = lax.rem(me + j, n_lon)
        copy = to_lon(
            peer, acc.at[pl.ds(peer * depth, depth)], landed.at[j], rs_send.at[j], rs_recv.at[j]
        )
        scatter.append(copy)
    tiles = groups * planes
    first = lax.rem(me + 1, n_lon) * depth
    start = jnp.minimum(first, tiles - 1) // planes

    def ready(peer):
        a = jnp.minimum(peer * depth, tiles - 1) // planes
        c = jnp.minimum(peer * depth + depth - 1, tiles - 1) // planes
        cut = jnp.logical_and(a < start, start <= c)
        return jnp.where(cut, groups - 1, lax.rem(c - start + groups, groups))

    def one_group(step, carry):
        g = lax.rem(start + step, groups)
        zsum = [jnp.zeros((GROUP, rows), F32) for _ in range(BASINS)]
        hsum = [jnp.zeros((GROUP, rows), F32) for _ in range(BASINS)]
        for pair in range(GROUP // 2):
            held = []
            for half in range(2):
                i = 2 * pair + half
                k = g * GROUP + i
                live = k < live_tally[...]
                f = jnp.where(live, flux[k].astype(F32), 0.0)
                t = warm[k].astype(F32)
                up = jnp.where(last_row, strip[k].astype(F32)[0:1], pltpu.roll(t, rows - 1, 0))
                high, low = split(f * (t + up))
                fb = f.astype(BF16)
                held.append(fb)
                pick = (slot == i).astype(F32).astype(BF16)
                for b in range(BASINS):
                    m = masks[b]
                    hsum[b] += nt_dot(pick, jnp.concatenate([high * m, low * m], axis=1))
            pick = (slot == 2 * pair + lane_half).astype(F32).astype(BF16)
            for b in range(BASINS):
                m = masks[b]
                zsum[b] += nt_dot(pick, jnp.concatenate([held[0] * m, held[1] * m], axis=1))
        for b in range(BASINS):
            acc[g * planes + b] = zsum[b] * scale_x
            acc[g * planes + BASINS + b] = hsum[b] * (0.5 * scale_x)
        for j in range(1, n_lon):
            pl.when(step == ready(lax.rem(me + j, n_lon)))(scatter[j - 1].start)
        return carry

    pl.when(me_lat < n_lat - 1)(strip_copy.wait_recv)
    for pair in loads:
        for copy in pair:
            copy.wait()
    lax.fori_loop(0, groups, one_group, 0)

    total = acc[pl.ds(me * depth, depth)]
    for j in range(1, n_lon):
        scatter[j - 1].wait_recv()
        total = total + landed[j]
    mine_out = reduced.at[pl.ds(me * depth, depth)]
    mine_out[...] = total
    half = n_lon // 2

    def lon_at(p):
        p = lax.rem(p + 2 * n_lon, n_lon)
        if n_lon % 2:
            return p
        return jnp.where(p < half, 2 * p, 2 * (n_lon - 1 - p) + 1)

    spot = me if n_lon % 2 else jnp.where(lax.rem(me, 2) == 0, me // 2, n_lon - 1 - me // 2)
    pieces = tuple((i * depth // 4, (i + 1) * depth // 4 - i * depth // 4) for i in range(4))
    gather = []
    for t in range(half):
        for c, (at, size) in enumerate(pieces):
            for way in ((1, -1) if t < n_lon - 1 - half else (1,)):
                if size == 0:
                    continue
                index = (t * 4 + c) * 2 + (way < 0)
                part = reduced.at[pl.ds(lon_at(spot - way * t) * depth + at, size)]
                copy = to_lon(lon_at(spot + way), part, part, ag_send.at[index], ag_recv.at[index])
                gather.append((t, c, way, copy))
    by_key = {(t, c, way): copy for t, c, way, copy in gather}
    for t, c, way, copy in gather:
        if t:
            by_key[t - 1, c, way].wait_recv()
        copy.start()
    for t, c, way, copy in gather:
        if (t + 1, c, way) not in by_key:
            copy.wait_recv()
    gather = [copy for _, _, _, copy in gather]

    sub = lax.broadcasted_iota(jnp.int32, (GROUP, rows), 0)
    for b in range(BASINS):
        above = jnp.zeros((1, rows), F32)
        for g in range(groups):
            x = reduced[g * planes + b]
            for by in (1, 2, 4):
                x = x + jnp.where(sub >= by, pltpu.roll(x, by, 0), 0.0)
            x = x + above
            above = x[GROUP - 1:GROUP]
            zonal[pl.ds((b * groups + g) * GROUP, GROUP), :] = x * scale_layers
    used = BASINS * groups * GROUP
    padded = zonal.shape[0]
    if padded > used:
        zonal[pl.ds(used, padded - used), :] = jnp.zeros((padded - used, rows), F32)
    high, low = split(zonal[...])
    ones = jnp.ones((GROUP, rows), BF16)
    totals[...] = nt_dot(ones, high) + nt_dot(ones, low)
    sends = []
    for j in range(1, n_lat):
        copy = pltpu.make_async_remote_copy(
            src_ref=totals, dst_ref=every.at[j], send_sem=tot_send.at[j], recv_sem=tot_recv.at[j],
            device_id={"lat": lax.rem(me_lat + j, n_lat)}, device_id_type=pl.DeviceIdType.MESH,
        )
        copy.start()
        sends.append(copy)
    upper = (
        lax.broadcasted_iota(jnp.int32, (rows, rows), 0)
        <= lax.broadcasted_iota(jnp.int32, (rows, rows), 1)
    ).astype(F32).astype(BF16)
    running = jnp.dot(high, upper, preferred_element_type=F32) + jnp.dot(
        low, upper, preferred_element_type=F32
    )
    height = groups * GROUP
    for b in range(BASINS):
        stream_out[b] = zonal[pl.ds(b * height, layers), :]
        for g in range(groups):
            size = min(GROUP, layers - g * GROUP)
            heat_out[b, pl.ds(g * GROUP, size), :] = reduced[g * planes + BASINS + b][:size]
    carried = jnp.zeros((GROUP, padded), F32)
    for j in range(1, n_lat):
        sends[j - 1].wait_recv()
        carried = carried + jnp.where(me_lat >= j, every[j], 0.0)
    blocks = []
    for i in range(padded // 128):
        line = carried[0:1, i * 128:(i + 1) * 128]
        blocks.append(jnp.broadcast_to(line, (128, 128)).T)
    spread = jnp.concatenate(blocks, axis=0)
    spread = jnp.concatenate([spread] * (rows // 128), axis=1)
    zonal[...] = (running + spread) * scale_y
    for b in range(BASINS):
        north_out[b] = zonal[pl.ds(b * height, layers), :]

    pl.when(me_lat > 0)(strip_copy.wait_send)
    for copy in scatter + gather + sends:
        copy.wait_send()


def on_device(
    northward_volume_flux, sheet_warmth, ocean_region_ids, ocean_grid_flags, thick_sheet_tally
):
    layers, rows, columns = northward_volume_flux.shape
    n_lat, n_lon = lax.axis_size("lat"), lax.axis_size("lon")
    scales = (
        1.0 / math.sqrt(columns * n_lon), 1.0 / math.sqrt(layers), 1.0 / math.sqrt(rows * n_lat)
    )
    groups = -(-layers // GROUP)
    tiles = groups * 2 * BASINS
    depth = -(-tiles // n_lon)
    padded = -(-BASINS * groups * GROUP // 128) * 128
    out = jax.ShapeDtypeStruct((BASINS, layers, rows), F32)
    anywhere = pl.BlockSpec(memory_space=pl.ANY)
    inside = pl.BlockSpec(memory_space=pltpu.VMEM)
    dma = pltpu.SemaphoreType.DMA
    return pl.pallas_call(
        functools.partial(kernel, n_lat, n_lon, layers, scales),
        out_shape=(out, out, out),
        in_specs=[anywhere, anywhere, inside, inside, inside],
        out_specs=(inside, inside, inside),
        scratch_shapes=[
            pltpu.VMEM((groups * GROUP, rows, columns), BF16),
            pltpu.VMEM((groups * GROUP, rows, columns), BF16),
            pltpu.VMEM((BASINS, rows, columns), BF16),
            pltpu.VMEM((rows, columns), jnp.int32),
            pltpu.VMEM((n_lon * depth, GROUP, rows), F32),
            pltpu.VMEM((n_lon, depth, GROUP, rows), F32),
            pltpu.VMEM((n_lon * depth, GROUP, rows), F32),
            pltpu.VMEM((groups * GROUP, 8, columns), BF16),
            pltpu.VMEM((padded, rows), F32),
            pltpu.VMEM((GROUP, padded), F32),
            pltpu.VMEM((n_lat, GROUP, padded), F32),
            dma((2, groups)),
            dma((n_lon,)), dma((n_lon,)), dma((4 * n_lon,)), dma((4 * n_lon,)),
            dma, dma,
            dma((n_lat,)), dma((n_lat,)),
        ],
        compiler_params=pltpu.CompilerParams(
            collective_id=0, has_side_effects=True, vmem_limit_bytes=60 * 1024 * 1024
        ),
        name="overturning",
    )(northward_volume_flux, sheet_warmth, ocean_region_ids, ocean_grid_flags, thick_sheet_tally)


def solution(mesh):
    placed = (
        P(None, "lat", "lon"),
        P(None, "lat", "lon"),
        P("lat", "lon"),
        P("lat", "lon"),
        P("lat", "lon"),
    )
    return jax.shard_map(
        on_device,
        mesh=mesh,
        in_specs=placed,
        out_specs=(P(None, None, "lat"), P(None, None, "lat"), P(None, None, "lat")),
        check_vma=False,
    )
```
